256 devices in a mesh: row: 16 (over x, y_lo, core), col: 8 (over z), slab: 2 (over y_hi).
Axes of the slice: x: 4, y: 4 (y_hi: 2, y_lo: 2; y = y_hi * 2 + y_lo), z: 8, core: 2. Of those that a mesh axis runs over, the one named last changes fastest.
Arguments:
- fields: bfloat16 [2, 16384, 1024], P(None, ('row', 'col', 'slab')), may hold values from -0.8984375 to 0.8984375
Outputs:
- gram: float32 [2, 16384, 16384], P(None, ('row', 'slab'), 'col')
The draws below stay inside these ranges and needn't reach their ends.
All inputs are finite; a program needn't handle non-finite values.
Results may differ from the reference program's by a relative error of at most 0.01.
Values may be sent and summed in bfloat16 or wider, within the bound.
A program may use at most 64 MiB of HBM per device.

```python
import jax
import jax.numpy as jnp
from jax import lax

PIX = 1024
NE = 16384
ROWB = 1024
KBLOCK = 128
N_ROW = 16
N_COL = 8
N_SLAB = 2


def block_levels(stream_key, shape, split, low, largest):
    loudness, own = 1.0, jax.random.fold_in(stream_key, 6)
    for axis_at, blocks in split:
        steps = jnp.exp(jax.random.uniform(jax.random.fold_in(own, axis_at), (blocks,), jnp.float32, low / len(split), largest / len(split)))
        loudness = loudness * jnp.repeat(steps, shape[axis_at] // blocks).reshape([-1 if axis == axis_at else 1 for axis in range(len(shape))])
    return loudness


def bell_draw(key, dims, width, bound, split=(), held_as=jnp.bfloat16):
    drawn = jax.random.normal(key, dims, jnp.float32) * width
    if len(split) > 0:
        drawn = block_levels(key, dims, split, -0.22, 0.18) * drawn
    return jnp.clip(drawn, min=-bound, max=bound).astype(held_as)


def setup_inputs(seed: int = 0) -> dict:
    key_of = jax.random.split(jax.random.key(seed), 2)
    return {
        "fields": bell_draw(key_of[0], (2, NE, PIX), 0.15, 0.8984375, ((1, 256),)),
    }


def pair_block(left, right):
    real = jnp.dot(left[0], right[0].T, precision=lax.Precision.HIGHEST) + jnp.dot(left[1], right[1].T, precision=lax.Precision.HIGHEST)
    imag = jnp.dot(left[0], right[1].T, precision=lax.Precision.HIGHEST) - jnp.dot(left[1], right[0].T, precision=lax.Precision.HIGHEST)
    return jnp.stack([real, imag])


def reference(fields):
    whole = fields.astype(jnp.float32)
    columns = whole.reshape(2, N_ROW, N_COL, KBLOCK, PIX).transpose(0, 2, 1, 3, 4).reshape(2, NE, PIX)
    half = PIX // N_SLAB
    block_rows = 512 if ROWB % 512 == 0 else ROWB
    blocks = whole.reshape(2, NE // block_rows, block_rows, PIX).transpose(1, 0, 2, 3)

    def one_block(rows_block):
        total = jnp.zeros((2, block_rows, NE), jnp.float32)
        for sub in range(N_SLAB):
            left = rows_block[:, :, sub * half:(sub + 1) * half]
            right = columns[:, :, sub * half:(sub + 1) * half]
            partial_sum = lax.optimization_barrier(pair_block(left, right).astype(jnp.bfloat16))
            total = total + partial_sum.astype(jnp.float32)
        return total

    result = lax.map(one_block, blocks)
    return result.transpose(1, 0, 2, 3).reshape(2, NE, NE)
```

```python
import jax
import jax.numpy as jnp
from jax import lax
from jax.experimental import pallas as pl
from jax.experimental.pallas import tpu as pltpu
from jax.sharding import PartitionSpec as P

MESH = pl.DeviceIdType.MESH
NT = (((1,), (1,)), ((), ()))
STEPS = (0, -1, 1, 2)
ELECTRON_OF_SLOT = (0, 3, 1, 2)


def kernel(f_ref, out_ref, cols, rows, neg, xy_send, xy_recv, d_send, d_recv, z_send, z_recv, own_sem):
    e, half = f_ref.shape[1], f_ref.shape[1] // 2
    r, z, s = lax.axis_index("row"), lax.axis_index("col"), lax.axis_index("slab")
    x, y_lo, core = r // 4, (r // 2) % 2, r % 2
    y = s * 2 + y_lo

    def at(x, y, z, core):
        return (x * 4 + (y % 2) * 2 + core, z, y // 2)

    to = {
        (0, 1): at((x + 1) % 4, y, z, core),
        (0, -1): at((x + 3) % 4, y, z, core),
        (1, 1): at(x, (y + 1) % 4, z, core),
        (1, -1): at(x, (y + 3) % 4, z, core),
        (2, 1): at(x, y, (z + 1) % 8, core),
        (2, -1): at(x, y, (z + 7) % 8, core),
        "core": at(x, y, z, 1 - core),
    }

    barrier = pltpu.get_barrier_semaphore()
    for device in to.values():
        pl.semaphore_signal(barrier, inc=1, device_id=device, device_id_type=MESH)
    pl.semaphore_wait(barrier, len(to))

    def piece(dx, dy):
        px, py = (x + dx + 4) % 4, (y + dy + 4) % 4
        return (px * 4 + (py % 2) * 2 + core) * 2 + py // 2

    def offset(plane, first, second):
        return (first, second) if plane == 0 else (second, first)

    def whole(plane, d):
        return cols.at[plane, piece(*d)]

    def part(plane, d, h):
        return cols.at[plane, piece(*d), pl.ds(h * half, half)]

    def source(plane, d):
        return f_ref.at[plane] if d == (0, 0) else whole(plane, d)

    def xy_copy(src, dst, device, index):
        return pltpu.make_async_remote_copy(
            src_ref=src, dst_ref=dst, send_sem=xy_send.at[0], recv_sem=xy_recv.at[index],
            device_id=device, device_id_type=MESH,
        )

    def send_whole(plane, d, axis, way, group):
        xy_copy(source(plane, d), whole(plane, d), to[(axis, way)], (plane * 5 + group) * 4 + (0 if way == 1 else 1)).start()

    def send_part(plane, d, h, axis, way, group):
        xy_copy(part(plane, d, h), part(plane, d, h), to[(axis, way)], (plane * 5 + group) * 4 + 2 + h).start()

    def hand_over(plane, d):
        pltpu.make_async_remote_copy(
            src_ref=source(plane, d), dst_ref=whole(plane, d), send_sem=d_send.at[0], recv_sem=d_recv.at[d[0] % 4],
            device_id=to["core"], device_id_type=MESH,
        ).start()

    def first_axis(plane):
        return 0 if plane == 0 else 1

    def spread(plane, i):
        d = offset(plane, STEPS[i], 0)
        for way in (1, -1):
            send_whole(plane, d, 1 - first_axis(plane), way, 1 + i)

    def take_wholes(plane, group):
        axis = first_axis(plane) if group == 0 else 1 - first_axis(plane)
        for kind, way in ((0, 1), (1, -1)):
            d = offset(plane, -way, 0) if group == 0 else offset(plane, STEPS[group - 1], -way)
            xy_copy(whole(plane, d), whole(plane, d), to["core"], (plane * 5 + group) * 4 + kind).wait_recv()
            send_part(plane, d, kind, axis, way, group)
            hand_over(plane, d)

    def take_parts(plane, group):
        d = offset(plane, 2, 0) if group == 0 else offset(plane, STEPS[group - 1], 2)
        for h in (0, 1):
            xy_copy(part(plane, d, h), part(plane, d, h), to["core"], (plane * 5 + group) * 4 + 2 + h).wait_recv()
        hand_over(plane, d)

    j = (z - 4 * s + 8) % 8
    places = (j, (11 - j) % 8)

    def slot_of(source_electron):
        c = source_electron
        return c + (c + 2) // 3 - 3 * (c // 3)

    def z_copy(way, n, src, dst, a):
        return pltpu.make_async_remote_copy(
            src_ref=src, dst_ref=dst, send_sem=z_send.at[way * 2 + a], recv_sem=z_recv.at[way * 16 + n],
            device_id=to[(2, 1 if way == 0 else -1)], device_id_type=MESH,
        )

    def rows_part(plane, other, slot, h):
        return rows.at[plane, other * 4 + slot, pl.ds(pl.multiple_of(h * half, half), half)]

    def z_own(other, parts):
        for way in (0, 1):
            @pl.when(places[way] < 4)
            def _():
                for i in parts:
                    plane, h = 1 - i // 2, i % 2
                    src = f_ref.at[plane, pl.ds(h * half, half)] if other == 0 else part(plane, (0, 2), h)
                    z_copy(way, other * 8 + i, src, rows_part(plane, other, slot_of(j), h), 0).start()

    def z_step(slot):
        for way in (0, 1):
            place = places[way]
            back = (place + 7) % 8
            far = back // 4
            n = slot - 2 * far * (back - 3) + (2 * (back // 7) if slot >= 14 else 0)
            other, a, i = n // 8, (n // 4) % 2, n % 4
            plane, h = 1 - i // 2, i % 2

            @pl.when((n >= 0) & (n < 16) & ((a == 0) | (place >= 2)))
            def _():
                origin = back - far * (back - 3) - a
                electron = origin if way == 0 else 3 - origin
                block = rows_part(plane, other, slot_of(electron), h)
                z_copy(way, n, block, block, 0).wait_recv()

                @pl.when((place >= 4) & (a == 0))
                def _():
                    z_copy(way, n, block, block, 0).start()

                @pl.when((place >= 4) & (place <= 6) & (a == 1))
                def _():
                    z_copy(way, n, block, block, 1).start()

                @pl.when((place >= 1) & (place <= 3) & (a == 0))
                def _():
                    z_copy(way, n + 4, block, block, 1).start()

    def wait_columns(dx):
        pltpu.make_async_copy(cols.at[0, pl.ds(0, 8)], cols.at[0, pl.ds(0, 8)], d_recv.at[dx % 4]).wait()

    def negate(slot, count):
        neg[pl.ds(slot, count)] = -rows[1, pl.ds(slot, count)]

    def multiply(slot, count, dx, start, width):
        m = count * e
        first = ((x + dx + 4) % 4) * 8 + start
        right_re = cols[0, pl.ds(first, width)].reshape(width * e, -1)
        right_im = cols[1, pl.ds(first, width)].reshape(width * e, -1)
        left_re = rows[0, pl.ds(slot, count)].reshape(m, -1)
        left_im = rows[1, pl.ds(slot, count)].reshape(m, -1)
        minus_im = neg[pl.ds(slot, count)].reshape(m, -1)
        sums = lax.dot_general(
            jnp.concatenate([left_re, minus_im]), right_re, NT, preferred_element_type=jnp.float32
        ) + lax.dot_general(jnp.concatenate([left_im, left_re]), right_im, NT, preferred_element_type=jnp.float32)
        lanes = pl.ds(pl.multiple_of(first * e, 128), width * e)
        for i in range(count):
            other, electron = (slot + i) // 4, ELECTRON_OF_SLOT[(slot + i) % 4]
            low = pl.multiple_of(electron * 2 * e + (s if other == 0 else 1 - s) * e, e)
            for plane in (0, 1):
                out_ref[plane, pl.ds(low, e), lanes] = sums[plane * m + i * e : plane * m + (i + 1) * e]

    here = (0, 0)
    z_own(0, (0, 1, 2, 3))
    for plane in (0, 1):
        for way in (1, -1):
            send_whole(plane, here, first_axis(plane), way, 0)
    for plane in (0, 1):
        spread(plane, 0)
    for plane in (0, 1):
        hand_over(plane, here)
    own = [pltpu.make_async_copy(f_ref.at[plane], whole(plane, here), own_sem.at[plane]) for plane in (0, 1)]
    for copy in own:
        copy.start()

    @pl.when(j < 4)
    def _():
        for plane in (0, 1):
            rows[plane, slot_of(j)] = f_ref[plane]

    z_step(0)
    z_step(1)
    for plane in (0, 1):
        take_wholes(plane, 0)
    for plane in (0, 1):
        spread(plane, 1)
    z_step(2)
    z_step(3)
    for plane in (0, 1):
        take_wholes(plane, 1)
    for plane in (0, 1):
        spread(plane, 2)
    z_step(4)
    for plane in (0, 1):
        take_parts(plane, 0)
    z_own(1, (0, 1))
    for plane in (0, 1):
        spread(plane, 3)
    z_step(5)
    z_step(6)
    for plane in (0, 1):
        take_wholes(plane, 2)
    z_step(7)
    for plane in (0, 1):
        take_parts(plane, 1)
    z_own(1, (2, 3))

    @pl.when(j < 4)
    def _():
        for plane in (0, 1):
            rows[plane, 4 + slot_of(j)] = cols[plane, piece(0, 2)]

    z_step(8)
    z_step(9)
    for plane in (0, 1):
        take_wholes(plane, 3)
    z_step(10)
    z_step(11)
    for plane in (0, 1):
        take_wholes(plane, 4)
    z_step(12)
    for plane in (0, 1):
        take_parts(plane, 2)
    z_step(13)
    for plane in (0, 1):
        take_parts(plane, 3)
    for copy in own:
        copy.wait()
    negate(0, 4)
    wait_columns(0)
    multiply(0, 4, 0, 0, 4)
    z_step(14)
    for plane in (0, 1):
        take_parts(plane, 4)
    multiply(0, 4, 0, 4, 4)
    for i, dx in ((1, -1), (2, 1), (3, 2)):
        z_step(14 + i)
        wait_columns(dx)
        multiply(0, 4, dx, 0, 4)
        multiply(0, 4, dx, 4, 4)
    negate(4, 2)
    for i, dx in enumerate(STEPS):
        z_step(18 + i)
        multiply(4, 2, dx, 0, 8)
    negate(6, 2)
    for dx in STEPS:
        multiply(6, 2, dx, 0, 8)

    def drain(blocks, sem):
        pltpu.make_async_copy(cols.at[0, pl.ds(0, blocks)], cols.at[0, pl.ds(0, blocks)], sem).wait()

    drain(30, xy_send.at[0])
    drain(32, d_send.at[0])
    for way in (0, 1):
        drain(4, z_send.at[way * 2])

        @pl.when((places[way] >= 1) & (places[way] <= 6))
        def _():
            drain(4, z_send.at[way * 2 + 1])


def body(fields):
    e, pixels = fields.shape[1], fields.shape[2]
    return pl.pallas_call(
        kernel,
        out_shape=jax.ShapeDtypeStruct((2, 8 * e, 32 * e), jnp.float32),
        in_specs=[pl.BlockSpec(memory_space=pltpu.VMEM)],
        out_specs=pl.BlockSpec(memory_space=pltpu.VMEM),
        scratch_shapes=[
            pltpu.VMEM((2, 32, e, pixels), jnp.bfloat16),
            pltpu.VMEM((2, 8, e, pixels), jnp.bfloat16),
            pltpu.VMEM((8, e, pixels), jnp.bfloat16),
            pltpu.SemaphoreType.DMA((1,)),
            pltpu.SemaphoreType.DMA((40,)),
            pltpu.SemaphoreType.DMA((1,)),
            pltpu.SemaphoreType.DMA((4,)),
            pltpu.SemaphoreType.DMA((4,)),
            pltpu.SemaphoreType.DMA((32,)),
            pltpu.SemaphoreType.DMA((2,)),
        ],
        compiler_params=pltpu.CompilerParams(collective_id=0, has_side_effects=True, vmem_limit_bytes=56 * 2**20),
        cost_estimate=pl.CostEstimate(flops=8 * 8 * e * 32 * e * pixels, bytes_accessed=2**23, transcendentals=0),
    )(fields)


def solution(mesh):
    placed = (P(None, ("row", "col", "slab"), None),)
    return jax.shard_map(
        body, mesh=mesh, in_specs=placed, out_specs=P(None, ("row", "slab"), "col"), check_vma=False
    )
```

```python
import jax
import jax.numpy as jnp
from jax import lax
from jax.experimental import pallas as pl
from jax.experimental.pallas import tpu as pltpu
from jax.sharding import PartitionSpec as P

MESH = pl.DeviceIdType.MESH
NT = (((1,), (1,)), ((), ()))
STEPS = (0, -1, 1, 2)
ELECTRON_OF_SLOT = (0, 3, 1, 2)
UNIT = 4
TAIL = 2
DIRECT = 1
SHIFT = (5, 2)
FIRST = {"wholes": (1, 3, 6, 9, 11), "parts": (4, 7, 9, 12, 14), "fourth": 6, "negate": (10, 14, 18)}
PRODUCTS = {
    10: ((0, 2, 0),), 14: ((2, 2, 0),), 15: ((0, 4, -1),), 16: ((0, 4, 1),), 17: ((0, 4, 2),),
    18: ((4, 2, 0),), 19: ((4, 2, -1),), 20: ((4, 2, 1),), 21: ((4, 2, 2),),
}


def is_end(place):
    return (1 - place // 4) * (1 - place * (3 - place) // 2)


def gather_kernel(f_ref, cols, rows, acc, neg, xy_send, xy_recv, d_send, d_recv, z_send, z_recv, z_tail, own_sem):
    e, half, quarter = f_ref.shape[1], f_ref.shape[1] // 2, f_ref.shape[1] * 2 // UNIT
    r, z, s = lax.axis_index("row"), lax.axis_index("col"), lax.axis_index("slab")
    x, y_lo, core = r // 4, (r // 2) % 2, r % 2
    y = s * 2 + y_lo

    def at(x, y, z, core):
        return (x * 4 + (y % 2) * 2 + core, z, y // 2)

    to = {
        (0, 1): at((x + 1) % 4, y, z, core),
        (0, -1): at((x + 3) % 4, y, z, core),
        (1, 1): at(x, (y + 1) % 4, z, core),
        (1, -1): at(x, (y + 3) % 4, z, core),
        (2, 1): at(x, y, (z + 1) % 8, core),
        (2, 2): at(x, y, (z + 2) % 8, core),
        (2, 3): at(x, y, (z + 3) % 8, core),
        (2, 4): at(x, y, (z + 4) % 8, core),
        (2, -1): at(x, y, (z + 7) % 8, core),
        (2, -2): at(x, y, (z + 6) % 8, core),
        (2, -3): at(x, y, (z + 5) % 8, core),
        "core": at(x, y, z, 1 - core),
    }

    barrier = pltpu.get_barrier_semaphore()
    for device in to.values():
        pl.semaphore_signal(barrier, inc=1, device_id=device, device_id_type=MESH)
    pl.semaphore_wait(barrier, len(to))

    def piece(dx, dy):
        px, py = (x + dx + 4) % 4, (y + dy + 4) % 4
        return (px * 4 + (py % 2) * 2 + core) * 2 + py // 2

    def offset(plane, first, second):
        return (first, second) if plane == 0 else (second, first)

    def whole(plane, d):
        return cols.at[plane, piece(*d)]

    def part(plane, d, h):
        return cols.at[plane, piece(*d), pl.ds(h * half, half)]

    def source(plane, d):
        return f_ref.at[plane] if d == (0, 0) else whole(plane, d)

    def xy_copy(src, dst, device, index):
        return pltpu.make_async_remote_copy(
            src_ref=src, dst_ref=dst, send_sem=xy_send.at[0], recv_sem=xy_recv.at[index],
            device_id=device, device_id_type=MESH,
        )

    def send_whole(plane, d, axis, way, group):
        xy_copy(source(plane, d), whole(plane, d), to[(axis, way)], (plane * 5 + group) * 4 + (0 if way == 1 else 1)).start()

    def send_part(plane, d, h, axis, way, group):
        xy_copy(part(plane, d, h), part(plane, d, h), to[(axis, way)], (plane * 5 + group) * 4 + 2 + h).start()

    def hand_over(plane, d):
        pltpu.make_async_remote_copy(
            src_ref=source(plane, d), dst_ref=whole(plane, d), send_sem=d_send.at[0], recv_sem=d_recv.at[d[0] % 4],
            device_id=to["core"], device_id_type=MESH,
        ).start()

    def first_axis(plane):
        return 0 if plane == 0 else 1

    def spread(plane, i):
        d = offset(plane, STEPS[i], 0)
        for way in (1, -1):
            send_whole(plane, d, 1 - first_axis(plane), way, 1 + i)

    def take_wholes(plane, group):
        axis = first_axis(plane) if group == 0 else 1 - first_axis(plane)
        for kind, way in ((0, 1), (1, -1)):
            d = offset(plane, -way, 0) if group == 0 else offset(plane, STEPS[group - 1], -way)
            xy_copy(whole(plane, d), whole(plane, d), to["core"], (plane * 5 + group) * 4 + kind).wait_recv()
            send_part(plane, d, kind, axis, way, group)
            hand_over(plane, d)

    def take_parts(plane, group):
        d = offset(plane, 2, 0) if group == 0 else offset(plane, STEPS[group - 1], 2)
        for h in (0, 1):
            xy_copy(part(plane, d, h), part(plane, d, h), to["core"], (plane * 5 + group) * 4 + 2 + h).wait_recv()
        hand_over(plane, d)

    j = (z - 4 * s + 8) % 8
    places = (j, (11 - j) % 8)

    def slot_of(c, place):
        return (c + (c + 2) // 3 - 3 * (c // 3) + 2 * is_end(place)) % 4

    def z_copy(way, n, src, dst, sem, hops=1):
        return pltpu.make_async_remote_copy(
            src_ref=src, dst_ref=dst, send_sem=sem, recv_sem=z_recv.at[way * 4 * UNIT + n],
            device_id=to[(2, hops if way == 0 or hops == 4 else -hops)], device_id_type=MESH,
        )

    def rows_part(plane, other, slot, q):
        return rows.at[plane, other * 4 + slot, pl.ds(pl.multiple_of(q * quarter, quarter), quarter)]

    def there(way, hops):
        return (j + (hops if way == 0 else 8 - hops)) % 8

    def z_own(other, planes):
        for way in (0, 1):
            @pl.when(places[way] < 4)
            def _():
                for i in range(UNIT):
                    plane, q = 1 - i // (UNIT // 2), i % (UNIT // 2)
                    if plane in planes:
                        src = f_ref.at[plane] if other == 0 else whole(plane, (0, 2))
                        z_copy(
                            way, other * 2 * UNIT + i, src.at[pl.ds(q * quarter, quarter)],
                            rows_part(plane, other, slot_of(j, there(way, 1)), q), z_send.at[way * 2],
                        ).start()

    def z_step(slot):
        last, direct = 4 * UNIT - TAIL, 4 * UNIT - DIRECT
        for way in (0, 1):
            place = places[way]
            back = (place + 7) % 8
            far = back // 4
            n = slot - SHIFT[0] * far * (back - 3) // SHIFT[1]
            other, a, i = n // (2 * UNIT), (n // UNIT) % 2, n % UNIT
            plane, q = 1 - i // (UNIT // 2), i % (UNIT // 2)

            @pl.when((n >= 0) & (n < 4 * UNIT) & ((a == 0) | (place >= 2)))
            def _():
                origin = back - far * (back - 3) - a
                electron = origin if way == 0 else 3 - origin
                block = rows_part(plane, other, slot_of(electron, j), q)
                z_copy(way, n, block, block, z_send.at[0]).wait_recv()

                def send(n, sem, hops=1):
                    to_block = rows_part(plane, other, slot_of(electron, there(way, hops)), q)
                    z_copy(way, n, block, to_block, sem, hops).start()

                @pl.when((place >= 4) & (a == 0))
                def _():
                    send(n, z_send.at[way * 2])

                @pl.when((place >= 4) & (place <= 6) & (a == 1) & (n < last))
                def _():
                    send(n, z_send.at[way * 2 + 1])

                @pl.when((place >= 1) & (place <= 3) & (a == 0) & ((place < 3) | (n < last - UNIT)))
                def _():
                    send(n + UNIT, z_send.at[way * 2 + 1])

                if slot >= last - UNIT:

                    @pl.when(((place == 4) | (place == 6)) & (n >= last) & (n < direct))
                    def _():
                        send(n, z_tail.at[way])

                    @pl.when((place == 3) & (a == 0) & (n >= last - UNIT))
                    def _():
                        send(n + UNIT, z_tail.at[way])
                        send(n + UNIT, z_tail.at[way], 3)

                        @pl.when(n >= direct - UNIT)
                        def _():
                            send(n + UNIT, z_tail.at[way], 2)
                            send(n + UNIT, z_tail.at[way], 4)

    def wait_columns(dx):
        pltpu.make_async_copy(cols.at[0, pl.ds(0, 8)], cols.at[0, pl.ds(0, 8)], d_recv.at[dx % 4]).wait()

    def negate(slot, count):
        neg[pl.ds(slot, count)] = -rows[1, pl.ds(slot, count)]

    def multiply(slot, count, dx, start, width):
        m = count * e
        first = ((x + dx + 4) % 4) * 8 + start
        right_re = cols[0, pl.ds(first, width)].reshape(width * e, -1)
        right_im = cols[1, pl.ds(first, width)].reshape(width * e, -1)
        left_re = rows[0, pl.ds(slot, count)].reshape(m, -1)
        left_im = rows[1, pl.ds(slot, count)].reshape(m, -1)
        minus_im = neg[pl.ds(slot, count)].reshape(m, -1)
        sums = lax.dot_general(
            jnp.concatenate([left_re, minus_im]), right_re, NT, preferred_element_type=jnp.float32
        ) + lax.dot_general(jnp.concatenate([left_im, left_re]), right_im, NT, preferred_element_type=jnp.float32)
        lanes = pl.ds(pl.multiple_of(first * e, 128), width * e)
        for plane in (0, 1):
            acc[plane, slot * e : slot * e + m, lanes] = sums[plane * m : (plane + 1) * m]

    def own_rows(plane):
        return pltpu.make_async_copy(f_ref.at[plane], rows.at[plane, slot_of(j, j)], own_sem.at[2 + plane])

    here = (0, 0)
    both = (0, 1)
    z_own(0, both)
    for plane in both:
        for way in (1, -1):
            send_whole(plane, here, first_axis(plane), way, 0)
    for plane in both:
        spread(plane, 0)
    for plane in both:
        hand_over(plane, here)
    own = [pltpu.make_async_copy(f_ref.at[plane], whole(plane, here), own_sem.at[plane]) for plane in both]
    for copy in own:
        copy.start()

    @pl.when(j < 4)
    def _():
        for plane in both:
            own_rows(plane).start()

    seen = set()

    def after(slot):
        if slot == FIRST["parts"][0]:
            for plane in both:
                take_parts(plane, 0)
            z_own(1, (1,))
        if slot in FIRST["wholes"]:
            group = FIRST["wholes"].index(slot)
            for plane in both:
                take_wholes(plane, group)
            if group < 2:
                for plane in both:
                    spread(plane, 1 + group)
        if slot == FIRST["fourth"]:
            for plane in both:
                spread(plane, 3)
        if slot in FIRST["parts"][1:]:
            group = FIRST["parts"].index(slot)
            for plane in both:
                take_parts(plane, group)
            if group == 1:
                z_own(1, (0,))

                @pl.when(j < 4)
                def _():
                    for plane in both:
                        rows[plane, 4 + slot_of(j, j)] = cols[plane, piece(0, 2)]

        if slot == FIRST["negate"][0]:
            for copy in own:
                copy.wait()

            @pl.when(j < 4)
            def _():
                for plane in both:
                    own_rows(plane).wait()

        if slot in FIRST["negate"]:
            negate(2 * FIRST["negate"].index(slot), 2)
        for low, count, dx in PRODUCTS.get(slot, ()):
            if dx not in seen:
                seen.add(dx)
                wait_columns(dx)
            multiply(low, count, dx, 0, 8)

    for slot in range(4 * UNIT + 3 * SHIFT[0] // SHIFT[1]):
        z_step(slot)
        after(slot)

    def drain(blocks, sem):
        pltpu.make_async_copy(cols.at[0, pl.ds(0, blocks)], cols.at[0, pl.ds(0, blocks)], sem).wait()

    drain(30, xy_send.at[0])
    drain(32, d_send.at[0])
    for way in (0, 1):
        drain(4, z_send.at[way * 2])

        @pl.when((places[way] == 1) | (places[way] == 2))
        def _():
            drain(4, z_send.at[way * 2 + 1])

        @pl.when((places[way] >= 3) & (places[way] <= 6))
        def _():
            drain(3, z_send.at[way * 2 + 1])

        @pl.when(places[way] == 3)
        def _():
            drain(3, z_tail.at[way])

        @pl.when((places[way] == 4) | (places[way] == 6))
        def _():
            pltpu.make_async_copy(part(0, here, 0), part(0, here, 0), z_tail.at[way]).wait()


def finish_kernel(cols, rows, acc, out, neg, last, acc_sem, last_sem):
    e = rows.shape[2]
    s = lax.axis_index("slab")

    at_end = is_end((lax.axis_index("col") - 4 * s + 8) % 8)

    def place(slot):
        side = s if slot < 4 else 1 - s
        plain, turned = ELECTRON_OF_SLOT[slot % 4], ELECTRON_OF_SLOT[(slot + 2) % 4]
        electron = plain + at_end * (turned - plain)
        return pl.ds(pl.multiple_of((electron * 2 + side) * e, e), e)

    copies = []
    for slot in range(6):
        for plane in (0, 1):
            copies.append(pltpu.make_async_copy(
                acc.at[plane, pl.ds(slot * e, e)], out.at[plane, place(slot)], acc_sem.at[slot * 2 + plane]
            ))
            copies[-1].start()
    m = 2 * e
    neg[...] = -rows[1, 6:8]
    left = jnp.concatenate([rows[0, 6:8].reshape(m, -1), neg[...].reshape(m, -1)])
    cross = jnp.concatenate([rows[1, 6:8].reshape(m, -1), rows[0, 6:8].reshape(m, -1)])
    for block in range(4):
        right_re = cols[0, block * 8 : block * 8 + 8].reshape(8 * e, -1)
        right_im = cols[1, block * 8 : block * 8 + 8].reshape(8 * e, -1)
        sums = lax.dot_general(left, right_re, NT, preferred_element_type=jnp.float32) + lax.dot_general(
            cross, right_im, NT, preferred_element_type=jnp.float32
        )
        for plane in (0, 1):
            last[plane, :, block * 8 * e : (block + 1) * 8 * e] = sums[plane * m : (plane + 1) * m]
            for i in (0, 1):
                lanes = pl.ds(block * 8 * e, 8 * e)
                copies.append(pltpu.make_async_copy(
                    last.at[plane, pl.ds(i * e, e), lanes], out.at[plane, place(6 + i), lanes],
                    last_sem.at[block * 4 + plane * 2 + i],
                ))
                copies[-1].start()
    for copy in copies:
        copy.wait()


def body(fields):
    e, pixels = fields.shape[1], fields.shape[2]
    vmem = pltpu.MemorySpace.VMEM
    cols, rows, acc = pl.pallas_call(
        gather_kernel,
        out_shape=(
            pltpu.VMEM((2, 32, e, pixels), jnp.bfloat16),
            pltpu.VMEM((2, 8, e, pixels), jnp.bfloat16),
            pltpu.VMEM((2, 6 * e, 32 * e), jnp.float32),
        ),
        in_specs=[pl.BlockSpec(memory_space=pltpu.MemorySpace.HBM)],
        out_specs=(pl.BlockSpec(memory_space=pltpu.VMEM),) * 3,
        scratch_shapes=[
            pltpu.VMEM((8, e, pixels), jnp.bfloat16),
            pltpu.SemaphoreType.DMA((1,)),
            pltpu.SemaphoreType.DMA((40,)),
            pltpu.SemaphoreType.DMA((1,)),
            pltpu.SemaphoreType.DMA((4,)),
            pltpu.SemaphoreType.DMA((4,)),
            pltpu.SemaphoreType.DMA((8 * UNIT,)),
            pltpu.SemaphoreType.DMA((2,)),
            pltpu.SemaphoreType.DMA((4,)),
        ],
        compiler_params=pltpu.CompilerParams(collective_id=0, has_side_effects=True, vmem_limit_bytes=20 * 2**20),
        cost_estimate=pl.CostEstimate(flops=6 * 8 * e * 32 * e * pixels, bytes_accessed=2**23, transcendentals=0),
    )(pltpu.with_memory_space_constraint(fields, pltpu.MemorySpace.HBM))
    cols, rows, acc = (pltpu.with_memory_space_constraint(a, vmem) for a in (cols, rows, acc))
    return pl.pallas_call(
        finish_kernel,
        out_shape=jax.ShapeDtypeStruct((2, 8 * e, 32 * e), jnp.float32),
        in_specs=[pl.BlockSpec(memory_space=pltpu.VMEM)] * 3,
        out_specs=pl.BlockSpec(memory_space=pl.ANY),
        scratch_shapes=[
            pltpu.VMEM((2, e, pixels), jnp.bfloat16),
            pltpu.VMEM((2, 2 * e, 32 * e), jnp.float32),
            pltpu.SemaphoreType.DMA((12,)),
            pltpu.SemaphoreType.DMA((16,)),
        ],
        compiler_params=pltpu.CompilerParams(vmem_limit_bytes=20 * 2**20),
        cost_estimate=pl.CostEstimate(flops=2 * 8 * e * 32 * e * pixels, bytes_accessed=2**23, transcendentals=0),
    )(cols, rows, acc)


def solution(mesh):
    placed = (P(None, ("row", "col", "slab"), None),)
    return jax.shard_map(
        body, mesh=mesh, in_specs=placed, out_specs=P(None, ("row", "slab"), "col"), check_vma=False
    )
```

```python
import jax
import jax.numpy as jnp
from jax import lax
from jax.experimental import pallas as pl
from jax.experimental.pallas import tpu as pltpu
from jax.sharding import PartitionSpec as P

MESH = pl.DeviceIdType.MESH
NT = (((1,), (1,)), ((), ()))
STEPS = (0, -1, 1, 2)
ELECTRON_OF_SLOT = (0, 3, 1, 2)
UNIT = 4
SHIFT = (5, 2)
FIRST = {"wholes": (1, 3, 6, 9, 11), "parts": (4, 7, 9, 12, 14), "fourth": 6, "negate": (10, 14, 18)}
PRODUCTS = {
    10: ((0, 2, 0),), 14: ((2, 2, 0),), 15: ((0, 4, -1),), 16: ((0, 4, 1),), 17: ((0, 4, 2),),
    18: ((4, 2, 0),), 19: ((4, 2, -1),), 20: ((4, 2, 1),), 21: ((4, 2, 2),),
}


def is_end(place):
    return (1 - place // 4) * (1 - place * (3 - place) // 2)


def gather_kernel(f_ref, cols, rows, acc, neg, xy_send, xy_recv, d_send, d_recv, z_send, z_recv, own_sem):
    e, half, quarter = f_ref.shape[1], f_ref.shape[1] // 2, f_ref.shape[1] * 2 // UNIT
    r, z, s = lax.axis_index("row"), lax.axis_index("col"), lax.axis_index("slab")
    x, y_lo, core = r // 4, (r // 2) % 2, r % 2
    y = s * 2 + y_lo

    def at(x, y, z, core):
        return (x * 4 + (y % 2) * 2 + core, z, y // 2)

    to = {
        (0, 1): at((x + 1) % 4, y, z, core),
        (0, -1): at((x + 3) % 4, y, z, core),
        (1, 1): at(x, (y + 1) % 4, z, core),
        (1, -1): at(x, (y + 3) % 4, z, core),
        (2, 1): at(x, y, (z + 1) % 8, core),
        (2, -1): at(x, y, (z + 7) % 8, core),
        "core": at(x, y, z, 1 - core),
    }

    barrier = pltpu.get_barrier_semaphore()
    for device in to.values():
        pl.semaphore_signal(barrier, inc=1, device_id=device, device_id_type=MESH)
    pl.semaphore_wait(barrier, len(to))

    def piece(dx, dy):
        px, py = (x + dx + 4) % 4, (y + dy + 4) % 4
        return (px * 4 + (py % 2) * 2 + core) * 2 + py // 2

    def offset(plane, first, second):
        return (first, second) if plane == 0 else (second, first)

    def whole(plane, d):
        return cols.at[plane, piece(*d)]

    def part(plane, d, h):
        return cols.at[plane, piece(*d), pl.ds(h * half, half)]

    def source(plane, d):
        return f_ref.at[plane] if d == (0, 0) else whole(plane, d)

    def xy_copy(src, dst, device, index):
        return pltpu.make_async_remote_copy(
            src_ref=src, dst_ref=dst, send_sem=xy_send.at[0], recv_sem=xy_recv.at[index],
            device_id=device, device_id_type=MESH,
        )

    def send_whole(plane, d, axis, way, group):
        xy_copy(source(plane, d), whole(plane, d), to[(axis, way)], (plane * 5 + group) * 4 + (0 if way == 1 else 1)).start()

    def send_part(plane, d, h, axis, way, group):
        xy_copy(part(plane, d, h), part(plane, d, h), to[(axis, way)], (plane * 5 + group) * 4 + 2 + h).start()

    def hand_over(plane, d):
        pltpu.make_async_remote_copy(
            src_ref=source(plane, d), dst_ref=whole(plane, d), send_sem=d_send.at[0], recv_sem=d_recv.at[d[0] % 4],
            device_id=to["core"], device_id_type=MESH,
        ).start()

    def first_axis(plane):
        return 0 if plane == 0 else 1

    def spread(plane, i):
        d = offset(plane, STEPS[i], 0)
        for way in (1, -1):
            send_whole(plane, d, 1 - first_axis(plane), way, 1 + i)

    def take_wholes(plane, group):
        axis = first_axis(plane) if group == 0 else 1 - first_axis(plane)
        for kind, way in ((0, 1), (1, -1)):
            d = offset(plane, -way, 0) if group == 0 else offset(plane, STEPS[group - 1], -way)
            xy_copy(whole(plane, d), whole(plane, d), to["core"], (plane * 5 + group) * 4 + kind).wait_recv()
            send_part(plane, d, kind, axis, way, group)
            hand_over(plane, d)

    def take_parts(plane, group):
        d = offset(plane, 2, 0) if group == 0 else offset(plane, STEPS[group - 1], 2)
        for h in (0, 1):
            xy_copy(part(plane, d, h), part(plane, d, h), to["core"], (plane * 5 + group) * 4 + 2 + h).wait_recv()
        hand_over(plane, d)

    j = (z - 4 * s + 8) % 8
    places = (j, (11 - j) % 8)

    def slot_of(c, place):
        return (c + (c + 2) // 3 - 3 * (c // 3) + 2 * is_end(place)) % 4

    def z_copy(way, n, src, dst, sem):
        return pltpu.make_async_remote_copy(
            src_ref=src, dst_ref=dst, send_sem=sem, recv_sem=z_recv.at[way * 4 * UNIT + n],
            device_id=to[(2, 1 - 2 * way)], device_id_type=MESH,
        )

    def rows_part(plane, other, slot, q):
        return rows.at[plane, other * 4 + slot, pl.ds(pl.multiple_of(q * quarter, quarter), quarter)]

    def there(way):
        return (j + (1 if way == 0 else 7)) % 8

    def z_own(other, planes):
        for way in (0, 1):
            @pl.when(places[way] < 4)
            def _():
                for i in range(UNIT):
                    plane, q = 1 - i // (UNIT // 2), i % (UNIT // 2)
                    if plane in planes:
                        src = f_ref.at[plane] if other == 0 else whole(plane, (0, 2))
                        z_copy(
                            way, other * 2 * UNIT + i, src.at[pl.ds(q * quarter, quarter)],
                            rows_part(plane, other, slot_of(j, there(way)), q), z_send.at[way * 2],
                        ).start()

    def z_step(slot):
        for way in (0, 1):
            place = places[way]
            back = (place + 7) % 8
            far = back // 4
            n = slot - SHIFT[0] * far * (back - 3) // SHIFT[1]
            other, a, i = n // (2 * UNIT), (n // UNIT) % 2, n % UNIT
            plane, q = 1 - i // (UNIT // 2), i % (UNIT // 2)

            @pl.when((n >= 0) & (n < 4 * UNIT) & ((a == 0) | (place >= 2)))
            def _():
                origin = back - far * (back - 3) - a
                electron = origin if way == 0 else 3 - origin
                block = rows_part(plane, other, slot_of(electron, j), q)
                z_copy(way, n, block, block, z_send.at[0]).wait_recv()

                def send(n, sem):
                    to_block = rows_part(plane, other, slot_of(electron, there(way)), q)
                    z_copy(way, n, block, to_block, sem).start()

                @pl.when((place >= 4) & (a == 0))
                def _():
                    send(n, z_send.at[way * 2])

                @pl.when((place >= 4) & (place <= 6) & (a == 1))
                def _():
                    send(n, z_send.at[way * 2 + 1])

                @pl.when((place >= 1) & (place <= 3) & (a == 0))
                def _():
                    send(n + UNIT, z_send.at[way * 2 + 1])


    def wait_columns(dx):
        pltpu.make_async_copy(cols.at[0, pl.ds(0, 8)], cols.at[0, pl.ds(0, 8)], d_recv.at[dx % 4]).wait()

    def negate(slot, count):
        neg[pl.ds(slot, count)] = -rows[1, pl.ds(slot, count)]

    def multiply(slot, count, dx, start, width):
        m = count * e
        first = ((x + dx + 4) % 4) * 8 + start
        right_re = cols[0, pl.ds(first, width)].reshape(width * e, -1)
        right_im = cols[1, pl.ds(first, width)].reshape(width * e, -1)
        left_re = rows[0, pl.ds(slot, count)].reshape(m, -1)
        left_im = rows[1, pl.ds(slot, count)].reshape(m, -1)
        minus_im = neg[pl.ds(slot, count)].reshape(m, -1)
        sums = lax.dot_general(
            jnp.concatenate([left_re, minus_im]), right_re, NT, preferred_element_type=jnp.float32
        ) + lax.dot_general(jnp.concatenate([left_im, left_re]), right_im, NT, preferred_element_type=jnp.float32)
        lanes = pl.ds(pl.multiple_of(first * e, 128), width * e)
        for plane in (0, 1):
            acc[plane, slot * e : slot * e + m, lanes] = sums[plane * m : (plane + 1) * m]

    def own_rows(plane):
        return pltpu.make_async_copy(f_ref.at[plane], rows.at[plane, slot_of(j, j)], own_sem.at[2 + plane])

    here = (0, 0)
    both = (0, 1)
    z_own(0, both)
    for plane in both:
        for way in (1, -1):
            send_whole(plane, here, first_axis(plane), way, 0)
    for plane in both:
        spread(plane, 0)
    for plane in both:
        hand_over(plane, here)
    own = [pltpu.make_async_copy(f_ref.at[plane], whole(plane, here), own_sem.at[plane]) for plane in both]
    for copy in own:
        copy.start()

    @pl.when(j < 4)
    def _():
        for plane in both:
            own_rows(plane).start()

    seen = set()

    def after(slot):
        if slot == FIRST["parts"][0]:
            for plane in both:
                take_parts(plane, 0)
            z_own(1, (1,))
        if slot in FIRST["wholes"]:
            group = FIRST["wholes"].index(slot)
            for plane in both:
                take_wholes(plane, group)
            if group < 2:
                for plane in both:
                    spread(plane, 1 + group)
        if slot == FIRST["fourth"]:
            for plane in both:
                spread(plane, 3)
        if slot in FIRST["parts"][1:]:
            group = FIRST["parts"].index(slot)
            for plane in both:
                take_parts(plane, group)
            if group == 1:
                z_own(1, (0,))

                @pl.when(j < 4)
                def _():
                    for plane in both:
                        rows[plane, 4 + slot_of(j, j)] = cols[plane, piece(0, 2)]

        if slot == FIRST["negate"][0]:
            for copy in own:
                copy.wait()

            @pl.when(j < 4)
            def _():
                for plane in both:
                    own_rows(plane).wait()

        if slot in FIRST["negate"]:
            negate(2 * FIRST["negate"].index(slot), 2)
        for low, count, dx in PRODUCTS.get(slot, ()):
            if dx not in seen:
                seen.add(dx)
                wait_columns(dx)
            multiply(low, count, dx, 0, 8)

    for slot in range(4 * UNIT + 3 * SHIFT[0] // SHIFT[1]):
        z_step(slot)
        after(slot)

    def drain(blocks, sem):
        pltpu.make_async_copy(cols.at[0, pl.ds(0, blocks)], cols.at[0, pl.ds(0, blocks)], sem).wait()

    drain(30, xy_send.at[0])
    drain(32, d_send.at[0])
    for way in (0, 1):
        drain(4, z_send.at[way * 2])

        @pl.when((places[way] >= 1) & (places[way] <= 6))
        def _():
            drain(4, z_send.at[way * 2 + 1])


def finish_kernel(cols, rows, acc, out, neg, last, acc_sem, last_sem):
    e = rows.shape[2]
    s = lax.axis_index("slab")

    at_end = is_end((lax.axis_index("col") - 4 * s + 8) % 8)

    def place(slot):
        side = s if slot < 4 else 1 - s
        plain, turned = ELECTRON_OF_SLOT[slot % 4], ELECTRON_OF_SLOT[(slot + 2) % 4]
        electron = plain + at_end * (turned - plain)
        return pl.ds(pl.multiple_of((electron * 2 + side) * e, e), e)

    copies = []
    for slot in range(6):
        for plane in (0, 1):
            copies.append(pltpu.make_async_copy(
                acc.at[plane, pl.ds(slot * e, e)], out.at[plane, place(slot)], acc_sem.at[slot * 2 + plane]
            ))
            copies[-1].start()
    m = 2 * e
    neg[...] = -rows[1, 6:8]
    left = jnp.concatenate([rows[0, 6:8].reshape(m, -1), neg[...].reshape(m, -1)])
    cross = jnp.concatenate([rows[1, 6:8].reshape(m, -1), rows[0, 6:8].reshape(m, -1)])
    for block in range(4):
        right_re = cols[0, block * 8 : block * 8 + 8].reshape(8 * e, -1)
        right_im = cols[1, block * 8 : block * 8 + 8].reshape(8 * e, -1)
        sums = lax.dot_general(left, right_re, NT, preferred_element_type=jnp.float32) + lax.dot_general(
            cross, right_im, NT, preferred_element_type=jnp.float32
        )
        for plane in (0, 1):
            last[plane, :, block * 8 * e : (block + 1) * 8 * e] = sums[plane * m : (plane + 1) * m]
            for i in (0, 1):
                lanes = pl.ds(block * 8 * e, 8 * e)
                copies.append(pltpu.make_async_copy(
                    last.at[plane, pl.ds(i * e, e), lanes], out.at[plane, place(6 + i), lanes],
                    last_sem.at[block * 4 + plane * 2 + i],
                ))
                copies[-1].start()
    for copy in copies:
        copy.wait()


def body(fields):
    e, pixels = fields.shape[1], fields.shape[2]
    vmem = pltpu.MemorySpace.VMEM
    cols, rows, acc = pl.pallas_call(
        gather_kernel,
        out_shape=(
            pltpu.VMEM((2, 32, e, pixels), jnp.bfloat16),
            pltpu.VMEM((2, 8, e, pixels), jnp.bfloat16),
            pltpu.VMEM((2, 6 * e, 32 * e), jnp.float32),
        ),
        in_specs=[pl.BlockSpec(memory_space=pltpu.MemorySpace.HBM)],
        out_specs=(pl.BlockSpec(memory_space=pltpu.VMEM),) * 3,
        scratch_shapes=[
            pltpu.VMEM((8, e, pixels), jnp.bfloat16),
            pltpu.SemaphoreType.DMA((1,)),
            pltpu.SemaphoreType.DMA((40,)),
            pltpu.SemaphoreType.DMA((1,)),
            pltpu.SemaphoreType.DMA((4,)),
            pltpu.SemaphoreType.DMA((4,)),
            pltpu.SemaphoreType.DMA((8 * UNIT,)),
            pltpu.SemaphoreType.DMA((4,)),
        ],
        compiler_params=pltpu.CompilerParams(collective_id=0, has_side_effects=True, vmem_limit_bytes=20 * 2**20),
        cost_estimate=pl.CostEstimate(flops=6 * 8 * e * 32 * e * pixels, bytes_accessed=2**23, transcendentals=0),
    )(pltpu.with_memory_space_constraint(fields, pltpu.MemorySpace.HBM))
    cols, rows, acc = (pltpu.with_memory_space_constraint(a, vmem) for a in (cols, rows, acc))
    return pl.pallas_call(
        finish_kernel,
        out_shape=jax.ShapeDtypeStruct((2, 8 * e, 32 * e), jnp.float32),
        in_specs=[pl.BlockSpec(memory_space=pltpu.VMEM)] * 3,
        out_specs=pl.BlockSpec(memory_space=pl.ANY),
        scratch_shapes=[
            pltpu.VMEM((2, e, pixels), jnp.bfloat16),
            pltpu.VMEM((2, 2 * e, 32 * e), jnp.float32),
            pltpu.SemaphoreType.DMA((12,)),
            pltpu.SemaphoreType.DMA((16,)),
        ],
        compiler_params=pltpu.CompilerParams(vmem_limit_bytes=20 * 2**20),
        cost_estimate=pl.CostEstimate(flops=2 * 8 * e * 32 * e * pixels, bytes_accessed=2**23, transcendentals=0),
    )(cols, rows, acc)


def solution(mesh):
    placed = (P(None, ("row", "col", "slab"), None),)
    return jax.shard_map(
        body, mesh=mesh, in_specs=placed, out_specs=P(None, ("row", "slab"), "col"), check_vma=False
    )
```

```python
import jax
import jax.numpy as jnp
from jax import lax
from jax.experimental import pallas as pl
from jax.experimental.pallas import tpu as pltpu
from jax.sharding import PartitionSpec as P

MESH = pl.DeviceIdType.MESH
NT = (((1,), (1,)), ((), ()))
STEPS = (0, -1, 1, 2)
ELECTRON_OF_SLOT = (0, 3, 1, 2)
UNIT = 8
SHIFT = (4, 1)
FIRST = {"wholes": (3, 7, 13, 19, 23), "parts": (10, 15, 20, 25, 29), "fourth": 13, "negate": (20, 28, 36)}
PRODUCTS = {
    20: ((0, 2, 0),), 28: ((2, 2, 0),), 30: ((0, 4, -1),), 32: ((0, 4, 1),), 34: ((0, 4, 2),),
    36: ((4, 2, 0),), 38: ((4, 2, -1),), 40: ((4, 2, 1),), 42: ((4, 2, 2),),
}


def is_end(place):
    return (1 - place // 4) * (1 - place * (3 - place) // 2)


def gather_kernel(f_ref, cols, rows, acc, neg, xy_send, xy_recv, d_send, d_recv, z_send, z_recv, own_sem):
    e, half, quarter = f_ref.shape[1], f_ref.shape[1] // 2, f_ref.shape[1] * 2 // UNIT
    r, z, s = lax.axis_index("row"), lax.axis_index("col"), lax.axis_index("slab")
    x, y_lo, core = r // 4, (r // 2) % 2, r % 2
    y = s * 2 + y_lo

    def at(x, y, z, core):
        return (x * 4 + (y % 2) * 2 + core, z, y // 2)

    to = {
        (0, 1): at((x + 1) % 4, y, z, core),
        (0, -1): at((x + 3) % 4, y, z, core),
        (1, 1): at(x, (y + 1) % 4, z, core),
        (1, -1): at(x, (y + 3) % 4, z, core),
        (2, 1): at(x, y, (z + 1) % 8, core),
        (2, -1): at(x, y, (z + 7) % 8, core),
        "core": at(x, y, z, 1 - core),
    }

    barrier = pltpu.get_barrier_semaphore()
    for device in to.values():
        pl.semaphore_signal(barrier, inc=1, device_id=device, device_id_type=MESH)
    pl.semaphore_wait(barrier, len(to))

    def piece(dx, dy):
        px, py = (x + dx + 4) % 4, (y + dy + 4) % 4
        return (px * 4 + (py % 2) * 2 + core) * 2 + py // 2

    def offset(plane, first, second):
        return (first, second) if plane == 0 else (second, first)

    def whole(plane, d):
        return cols.at[plane, piece(*d)]

    def part(plane, d, h):
        return cols.at[plane, piece(*d), pl.ds(h * half, half)]

    def source(plane, d):
        return f_ref.at[plane] if d == (0, 0) else whole(plane, d)

    def xy_copy(src, dst, device, index):
        return pltpu.make_async_remote_copy(
            src_ref=src, dst_ref=dst, send_sem=xy_send.at[0], recv_sem=xy_recv.at[index],
            device_id=device, device_id_type=MESH,
        )

    def send_whole(plane, d, axis, way, group):
        xy_copy(source(plane, d), whole(plane, d), to[(axis, way)], (plane * 5 + group) * 4 + (0 if way == 1 else 1)).start()

    def send_part(plane, d, h, axis, way, group):
        xy_copy(part(plane, d, h), part(plane, d, h), to[(axis, way)], (plane * 5 + group) * 4 + 2 + h).start()

    def hand_over(plane, d):
        pltpu.make_async_remote_copy(
            src_ref=source(plane, d), dst_ref=whole(plane, d), send_sem=d_send.at[0], recv_sem=d_recv.at[d[0] % 4],
            device_id=to["core"], device_id_type=MESH,
        ).start()

    def first_axis(plane):
        return 0 if plane == 0 else 1

    def spread(plane, i):
        d = offset(plane, STEPS[i], 0)
        for way in (1, -1):
            send_whole(plane, d, 1 - first_axis(plane), way, 1 + i)

    def take_wholes(plane, group):
        axis = first_axis(plane) if group == 0 else 1 - first_axis(plane)
        for kind, way in ((0, 1), (1, -1)):
            d = offset(plane, -way, 0) if group == 0 else offset(plane, STEPS[group - 1], -way)
            xy_copy(whole(plane, d), whole(plane, d), to["core"], (plane * 5 + group) * 4 + kind).wait_recv()
            send_part(plane, d, kind, axis, way, group)
            hand_over(plane, d)

    def take_parts(plane, group):
        d = offset(plane, 2, 0) if group == 0 else offset(plane, STEPS[group - 1], 2)
        for h in (0, 1):
            xy_copy(part(plane, d, h), part(plane, d, h), to["core"], (plane * 5 + group) * 4 + 2 + h).wait_recv()
        hand_over(plane, d)

    j = (z - 4 * s + 8) % 8
    places = (j, (11 - j) % 8)

    def slot_of(c, place):
        return (c + (c + 2) // 3 - 3 * (c // 3) + 2 * is_end(place)) % 4

    def z_copy(way, n, src, dst, sem):
        return pltpu.make_async_remote_copy(
            src_ref=src, dst_ref=dst, send_sem=sem, recv_sem=z_recv.at[way * 4 * UNIT + n],
            device_id=to[(2, 1 - 2 * way)], device_id_type=MESH,
        )

    def rows_part(plane, other, slot, q):
        return rows.at[plane, other * 4 + slot, pl.ds(pl.multiple_of(q * quarter, quarter), quarter)]

    def there(way):
        return (j + (1 if way == 0 else 7)) % 8

    def z_own(other, planes):
        for way in (0, 1):
            @pl.when(places[way] < 4)
            def _():
                for i in range(UNIT):
                    plane, q = 1 - i // (UNIT // 2), i % (UNIT // 2)
                    if plane in planes:
                        src = f_ref.at[plane] if other == 0 else whole(plane, (0, 2))
                        z_copy(
                            way, other * 2 * UNIT + i, src.at[pl.ds(q * quarter, quarter)],
                            rows_part(plane, other, slot_of(j, there(way)), q), z_send.at[way * 2],
                        ).start()

    def z_step(slot):
        for way in (0, 1):
            place = places[way]
            back = (place + 7) % 8
            far = back // 4
            n = slot - SHIFT[0] * far * (back - 3) // SHIFT[1]
            other, a, i = n // (2 * UNIT), (n // UNIT) % 2, n % UNIT
            plane, q = 1 - i // (UNIT // 2), i % (UNIT // 2)

            @pl.when((n >= 0) & (n < 4 * UNIT) & ((a == 0) | (place >= 2)))
            def _():
                origin = back - far * (back - 3) - a
                electron = origin if way == 0 else 3 - origin
                block = rows_part(plane, other, slot_of(electron, j), q)
                z_copy(way, n, block, block, z_send.at[0]).wait_recv()

                def send(n, sem):
                    to_block = rows_part(plane, other, slot_of(electron, there(way)), q)
                    z_copy(way, n, block, to_block, sem).start()

                @pl.when((place >= 4) & (a == 0))
                def _():
                    send(n, z_send.at[way * 2])

                @pl.when((place >= 4) & (place <= 6) & (a == 1))
                def _():
                    send(n, z_send.at[way * 2 + 1])

                @pl.when((place >= 1) & (place <= 3) & (a == 0))
                def _():
                    send(n + UNIT, z_send.at[way * 2 + 1])


    def wait_columns(dx):
        pltpu.make_async_copy(cols.at[0, pl.ds(0, 8)], cols.at[0, pl.ds(0, 8)], d_recv.at[dx % 4]).wait()

    def negate(slot, count):
        neg[pl.ds(slot, count)] = -rows[1, pl.ds(slot, count)]

    def multiply(slot, count, dx, start, width):
        m = count * e
        first = ((x + dx + 4) % 4) * 8 + start
        right_re = cols[0, pl.ds(first, width)].reshape(width * e, -1)
        right_im = cols[1, pl.ds(first, width)].reshape(width * e, -1)
        left_re = rows[0, pl.ds(slot, count)].reshape(m, -1)
        left_im = rows[1, pl.ds(slot, count)].reshape(m, -1)
        minus_im = neg[pl.ds(slot, count)].reshape(m, -1)
        sums = lax.dot_general(
            jnp.concatenate([left_re, minus_im]), right_re, NT, preferred_element_type=jnp.float32
        ) + lax.dot_general(jnp.concatenate([left_im, left_re]), right_im, NT, preferred_element_type=jnp.float32)
        lanes = pl.ds(pl.multiple_of(first * e, 128), width * e)
        for plane in (0, 1):
            acc[plane, slot * e : slot * e + m, lanes] = sums[plane * m : (plane + 1) * m]

    def own_rows(plane):
        return pltpu.make_async_copy(f_ref.at[plane], rows.at[plane, slot_of(j, j)], own_sem.at[2 + plane])

    here = (0, 0)
    both = (0, 1)
    z_own(0, both)
    for plane in both:
        for way in (1, -1):
            send_whole(plane, here, first_axis(plane), way, 0)
    for plane in both:
        spread(plane, 0)
    for plane in both:
        hand_over(plane, here)
    own = [pltpu.make_async_copy(f_ref.at[plane], whole(plane, here), own_sem.at[plane]) for plane in both]
    for copy in own:
        copy.start()

    @pl.when(j < 4)
    def _():
        for plane in both:
            own_rows(plane).start()

    seen = set()

    def after(slot):
        if slot == FIRST["parts"][0]:
            for plane in both:
                take_parts(plane, 0)
            z_own(1, (1,))
        if slot in FIRST["wholes"]:
            group = FIRST["wholes"].index(slot)
            for plane in both:
                take_wholes(plane, group)
            if group < 2:
                for plane in both:
                    spread(plane, 1 + group)
        if slot == FIRST["fourth"]:
            for plane in both:
                spread(plane, 3)
        if slot in FIRST["parts"][1:]:
            group = FIRST["parts"].index(slot)
            for plane in both:
                take_parts(plane, group)
            if group == 1:
                z_own(1, (0,))

                @pl.when(j < 4)
                def _():
                    for plane in both:
                        rows[plane, 4 + slot_of(j, j)] = cols[plane, piece(0, 2)]

        if slot == FIRST["negate"][0]:
            for copy in own:
                copy.wait()

            @pl.when(j < 4)
            def _():
                for plane in both:
                    own_rows(plane).wait()

        if slot in FIRST["negate"]:
            negate(2 * FIRST["negate"].index(slot), 2)
        for low, count, dx in PRODUCTS.get(slot, ()):
            if dx not in seen:
                seen.add(dx)
                wait_columns(dx)
            multiply(low, count, dx, 0, 8)

    for slot in range(4 * UNIT + 3 * SHIFT[0] // SHIFT[1]):
        z_step(slot)
        after(slot)

    def drain(blocks, sem):
        pltpu.make_async_copy(cols.at[0, pl.ds(0, blocks)], cols.at[0, pl.ds(0, blocks)], sem).wait()

    drain(30, xy_send.at[0])
    drain(32, d_send.at[0])
    for way in (0, 1):
        drain(4, z_send.at[way * 2])

        @pl.when((places[way] >= 1) & (places[way] <= 6))
        def _():
            drain(4, z_send.at[way * 2 + 1])


def finish_kernel(cols, rows, acc, out, neg, last, acc_sem, last_sem):
    e = rows.shape[2]
    s = lax.axis_index("slab")

    at_end = is_end((lax.axis_index("col") - 4 * s + 8) % 8)

    def place(slot):
        side = s if slot < 4 else 1 - s
        plain, turned = ELECTRON_OF_SLOT[slot % 4], ELECTRON_OF_SLOT[(slot + 2) % 4]
        electron = plain + at_end * (turned - plain)
        return pl.ds(pl.multiple_of((electron * 2 + side) * e, e), e)

    copies = []
    for slot in range(6):
        for plane in (0, 1):
            copies.append(pltpu.make_async_copy(
                acc.at[plane, pl.ds(slot * e, e)], out.at[plane, place(slot)], acc_sem.at[slot * 2 + plane]
            ))
            copies[-1].start()
    m = 2 * e
    neg[...] = -rows[1, 6:8]
    left = jnp.concatenate([rows[0, 6:8].reshape(m, -1), neg[...].reshape(m, -1)])
    cross = jnp.concatenate([rows[1, 6:8].reshape(m, -1), rows[0, 6:8].reshape(m, -1)])
    for block, (low, width) in enumerate(((0, 16), (16, 8), (24, 8))):
        right_re = cols[0, low : low + width].reshape(width * e, -1)
        right_im = cols[1, low : low + width].reshape(width * e, -1)
        sums = lax.dot_general(left, right_re, NT, preferred_element_type=jnp.float32) + lax.dot_general(
            cross, right_im, NT, preferred_element_type=jnp.float32
        )
        for plane in (0, 1):
            last[plane, :, low * e : (low + width) * e] = sums[plane * m : (plane + 1) * m]
            for i in (0, 1):
                lanes = pl.ds(low * e, width * e)
                copies.append(pltpu.make_async_copy(
                    last.at[plane, pl.ds(i * e, e), lanes], out.at[plane, place(6 + i), lanes],
                    last_sem.at[block * 4 + plane * 2 + i],
                ))
                copies[-1].start()
    for copy in copies:
        copy.wait()


def body(fields):
    e, pixels = fields.shape[1], fields.shape[2]
    vmem = pltpu.MemorySpace.VMEM
    cols, rows, acc = pl.pallas_call(
        gather_kernel,
        out_shape=(
            pltpu.VMEM((2, 32, e, pixels), jnp.bfloat16),
            pltpu.VMEM((2, 8, e, pixels), jnp.bfloat16),
            pltpu.VMEM((2, 6 * e, 32 * e), jnp.float32),
        ),
        in_specs=[pl.BlockSpec(memory_space=pltpu.MemorySpace.HBM)],
        out_specs=(pl.BlockSpec(memory_space=pltpu.VMEM),) * 3,
        scratch_shapes=[
            pltpu.VMEM((8, e, pixels), jnp.bfloat16),
            pltpu.SemaphoreType.DMA((1,)),
            pltpu.SemaphoreType.DMA((40,)),
            pltpu.SemaphoreType.DMA((1,)),
            pltpu.SemaphoreType.DMA((4,)),
            pltpu.SemaphoreType.DMA((4,)),
            pltpu.SemaphoreType.DMA((8 * UNIT,)),
            pltpu.SemaphoreType.DMA((4,)),
        ],
        compiler_params=pltpu.CompilerParams(collective_id=0, has_side_effects=True, vmem_limit_bytes=20 * 2**20),
        cost_estimate=pl.CostEstimate(flops=6 * 8 * e * 32 * e * pixels, bytes_accessed=2**23, transcendentals=0),
    )(pltpu.with_memory_space_constraint(fields, pltpu.MemorySpace.HBM))
    cols, rows, acc = (pltpu.with_memory_space_constraint(a, vmem) for a in (cols, rows, acc))
    return pl.pallas_call(
        finish_kernel,
        out_shape=jax.ShapeDtypeStruct((2, 8 * e, 32 * e), jnp.float32),
        in_specs=[pl.BlockSpec(memory_space=pltpu.VMEM)] * 3,
        out_specs=pl.BlockSpec(memory_space=pl.ANY),
        scratch_shapes=[
            pltpu.VMEM((2, e, pixels), jnp.bfloat16),
            pltpu.VMEM((2, 2 * e, 32 * e), jnp.float32),
            pltpu.SemaphoreType.DMA((12,)),
            pltpu.SemaphoreType.DMA((12,)),
        ],
        compiler_params=pltpu.CompilerParams(vmem_limit_bytes=20 * 2**20),
        cost_estimate=pl.CostEstimate(flops=2 * 8 * e * 32 * e * pixels, bytes_accessed=2**23, transcendentals=0),
    )(cols, rows, acc)


def solution(mesh):
    placed = (P(None, ("row", "col", "slab"), None),)
    return jax.shard_map(
        body, mesh=mesh, in_specs=placed, out_specs=P(None, ("row", "slab"), "col"), check_vma=False
    )
```
